32 devices in a mesh: ctx: 8 (over y, x, core), batch: 4 (over z).
Axes of the slice: x: 2, y: 2, z: 4, core: 2. Of those that a mesh axis runs over, the one named last changes fastest.
Arguments:
- queries: bfloat16 [12288, 6144], P(('batch', 'ctx')), parts along dimension 0, may hold values from -8 to 8
- keys: bfloat16 [12288, 384], P(('batch', 'ctx')), parts along dimension 0, may hold values from -8 to 8
- values: bfloat16 [12288, 256], P(('batch', 'ctx')), parts along dimension 0, may hold values from -15 to 15
- selected: int32 [192, 2, 16], P(('batch', 'ctx')), parts along dimension 0, may hold values from -1 to 47, as said below
Outputs:
- attended: bfloat16 [12288, 4096], P(('batch', 'ctx')), parts along dimension 0
The draws below stay inside these ranges and needn't reach their ends.
There are 4 independent parts, one for each index of `batch`. The reference program is written for one: setup_inputs(seed, part) draws one part's arguments, and reference() takes and returns one part's arrays. A program takes and returns all parts, laid end to end along the dimension named above; each array names one. Nothing has to cross between parts.
Inputs may be any that keep to these rules, and one draw needn't show every extreme that they name: `selected`: row b, group g lists distinct blocks c <= b in any order, -1 in the unused slots; blocks 0, b and b - 1 are always listed.
All inputs are finite; a program needn't handle non-finite values.
Results may differ from the reference program's by a relative error of at most 0.0048.
Values may be sent and summed in bfloat16 or wider, within the bound.
No kernel may reach another device: no remote copies, remote signals or barrier semaphores. Data moves between devices by JAX's collectives and lax.ppermute only.
A program may use at most 128 MiB of HBM per device.

```python
import math
import jax
import jax.numpy as jnp
from jax import lax

D_HEAD = 192
D_VALUE = 128
HEADS = 32
GROUPS = 2
BLOCK = 64
SELECT = 16
TOKENS = 3072


def draw_queries(key, part):
    shape = (TOKENS, HEADS * D_HEAD)
    base_draw = jnp.clip(1.2 * jax.random.normal(jax.random.fold_in(key, 1), shape, jnp.float32), -8.0, 8.0)
    return base_draw.astype(jnp.bfloat16)


def draw_keys(key, part):
    shape = (TOKENS, GROUPS * D_HEAD)
    base_draw = jnp.clip(jax.random.normal(jax.random.fold_in(key, 2), shape, jnp.float32), -8.0, 8.0)
    return base_draw.astype(jnp.bfloat16)


def draw_selected(key, part):
    blocks = TOKENS // BLOCK
    second_key = jax.random.fold_in(key, 12)
    query_blk = jnp.arange(blocks, dtype=jnp.int32)[:, None, None]
    cand_blk = jnp.arange(blocks, dtype=jnp.int32)[None, None, :]
    causal = cand_blk <= query_blk
    candidate = cand_blk < query_blk
    must_list = causal & ((cand_blk == 0) | (cand_blk == query_blk) | (cand_blk == query_blk - 1))
    rand_part = jax.random.randint(second_key, (blocks, GROUPS, blocks), 0, 2 ** 16)
    recency = 2 ** 18 // jnp.maximum(1 + query_blk - cand_blk, 1)
    ranked = (rand_part + recency) * blocks + cand_blk
    ranked = jnp.where(must_list, 2 ** 30 + cand_blk, jnp.where(candidate, ranked, -1))
    top_vals, top_index = lax.top_k(ranked, SELECT)
    return jnp.where(top_vals >= 0, top_index, -1).astype(jnp.int32)


def level_of(own_key, extent, split, low, largest):
    def one(axis_at, blocks):
        steps = jax.random.uniform(jax.random.fold_in(jax.random.fold_in(own_key, 6), axis_at), (blocks,), jnp.float32, low / len(split), largest / len(split))
        return jnp.repeat(jnp.exp(steps), extent[axis_at] // blocks).reshape((-1,) + (1,) * (len(extent) - axis_at - 1))

    level = one(*split[0])
    for cut in split[1:]:
        level = level * one(*cut)
    return level


def noise(own_key, dims, scale, bound, pieces=(), kind=jnp.bfloat16):
    drawn = jax.random.normal(own_key, dims, jnp.float32) * scale
    if len(pieces) > 0:
        drawn = level_of(own_key, dims, pieces, -0.22, 0.18) * drawn
    return jnp.clip(drawn, min=-bound, max=bound).astype(kind)


def setup_inputs(seed: int = 0, part: int = 0) -> dict:
    key_of = jax.random.split(jax.random.key(seed), 5)
    own_keys = jax.random.split(jax.random.fold_in(key_of[4], part), 5)
    return {
        "queries": draw_queries(jax.random.fold_in(jax.random.fold_in(key_of[4], part), 71), part),
        "keys": draw_keys(jax.random.fold_in(jax.random.fold_in(key_of[4], part), 71), part),
        "values": noise(own_keys[2], (TOKENS, GROUPS * D_VALUE), 3.0, 15.0, ((0, 8),)),
        "selected": draw_selected(jax.random.fold_in(jax.random.fold_in(key_of[4], part), 71), part),
    }


def attend_exact(qblock, near_keys, near_values, chosen, block_index):
    groups, slot_count, block_len, head_dim = near_keys.shape
    value_dim = near_values.shape[3]
    key_rows = near_keys.reshape(groups, slot_count * block_len, head_dim).astype(jnp.float32)
    value_rows = near_values.reshape(groups, slot_count * block_len, value_dim).astype(jnp.float32)
    scores = jnp.einsum('qghd,gkd->gqhk', qblock.astype(jnp.float32), key_rows) * (1.0 / math.sqrt(head_dim))
    offsets = jnp.arange(block_len, dtype=jnp.int32)
    key_pos = (jnp.maximum(chosen, 0)[:, :, None] * block_len + offsets[None, None, :]).reshape(groups, -1)
    listed = jnp.broadcast_to((chosen >= 0)[:, :, None], (groups, slot_count, block_len)).reshape(groups, -1)
    query_pos = block_index * block_len + offsets
    allowed = listed[:, None, :] & (key_pos[:, None, :] <= query_pos[None, :, None])
    allowed = allowed[:, :, None, :]
    masked = jnp.where(allowed, scores, jnp.float32(-1e+30))
    row_max = lax.optimization_barrier(jnp.max(masked, axis=-1, keepdims=True))
    exp_terms = jnp.where(allowed, jnp.exp(masked - row_max), jnp.float32(0.0))
    row_sum = lax.optimization_barrier(jnp.sum(exp_terms, axis=-1, keepdims=True))
    weights = (exp_terms / row_sum).astype(jnp.bfloat16)
    result = jnp.einsum('gqhk,gkd->qghd', weights.astype(jnp.float32), value_rows)
    return result.astype(jnp.bfloat16).reshape(block_len, -1)

def reference(queries, keys, values, selected):
    blocks = TOKENS // BLOCK
    heads_per = HEADS // GROUPS
    query_blocks = queries.reshape(blocks, BLOCK, GROUPS, heads_per, D_HEAD)
    key_table = keys.reshape(blocks, BLOCK, GROUPS, D_HEAD).transpose(0, 2, 1, 3)
    value_table = values.reshape(blocks, BLOCK, GROUPS, D_VALUE).transpose(0, 2, 1, 3)
    group_ids = jnp.arange(GROUPS, dtype=jnp.int32)[:, None]

    def per_block(inputs):
        block_index, qblock, chosen = inputs
        picks = jnp.maximum(chosen, 0).astype(jnp.int32)
        return attend_exact(qblock, key_table[picks, group_ids], value_table[picks, group_ids], chosen, block_index)
    result = lax.map(per_block, (jnp.arange(blocks, dtype=jnp.int32), query_blocks, selected))
    return result.reshape(TOKENS, HEADS * D_VALUE)
```

```python
import functools
import math

import jax
import jax.numpy as jnp
from jax import lax
from jax.experimental import pallas as pl
from jax.experimental.pallas import tpu as pltpu
from jax.sharding import PartitionSpec as P

D_HEAD = 192
D_VALUE = 128
BLOCK = 64
LANES = 128
HALF = 64
NEG = -1e30


def attend_kernel(picks, queries, *refs, pieces, groups, heads_per, slots, chunk):
    key_pieces = refs[:pieces]
    value_pieces = refs[pieces : 2 * pieces]
    out, keys, values, near_keys, near_values, near_queries, sems = refs[2 * pieces :]
    step = pl.program_id(0)
    steps = pl.num_programs(0)
    tok_rows = key_pieces[0].shape[0]

    @pl.when(step == 0)
    def _():
        copies = []
        for j in range(pieces):
            copies.append(pltpu.make_async_copy(key_pieces[j], keys.at[j], sems.at[0, j]))
            copies.append(pltpu.make_async_copy(value_pieces[j], values.at[j], sems.at[1, j]))
        for copy in copies:
            copy.start()
        near_values[:, :, D_VALUE:] = jnp.ones((groups, slots * BLOCK, LANES), jnp.bfloat16)
        for copy in copies:
            copy.wait()

    my_index = picks[steps * groups * slots]
    block = my_index * steps + step
    lane = lax.broadcasted_iota(jnp.int32, (BLOCK, LANES), 1)
    row = lax.broadcasted_iota(jnp.int32, (BLOCK, LANES), 0)
    low = lane < HALF
    own_row = (lane % HALF == row).astype(jnp.bfloat16)
    causal = jnp.where(row > lane % HALF, NEG, 0.0).astype(jnp.float32)

    def rolled(x):
        return pltpu.roll(x.astype(jnp.float32), HALF, 1).astype(jnp.bfloat16)

    for g in range(groups):
        for s in range(slots):
            pick = picks[(step * groups + g) * slots + s]
            listed = jnp.maximum(pick, 0)
            piece = (listed // steps) ^ my_index
            at = pl.ds(pl.multiple_of((listed % steps) * BLOCK, BLOCK), BLOCK)
            bias = jnp.where(pick == block, causal, jnp.where(pick < 0, NEG, 0.0).astype(jnp.float32))
            bias = bias.astype(jnp.bfloat16)
            to = slice(s * BLOCK, (s + 1) * BLOCK)
            if g == 0:
                near_keys[g, to, :LANES] = keys[piece, at, :LANES]
                near_keys[g, to, LANES:] = jnp.where(low, keys[piece, at, LANES : 2 * LANES], bias)
            else:
                near_keys[g, to, :LANES] = jnp.where(low, bias, keys[piece, at, LANES : 2 * LANES])
                near_keys[g, to, LANES:] = keys[piece, at, 2 * LANES :]
            near_values[g, to, :D_VALUE] = values[piece, at, g * D_VALUE : (g + 1) * D_VALUE]
        for h in range(0, heads_per, 2):
            col = (g * heads_per + h) * D_HEAD
            q0 = queries[:, col : col + LANES]
            q1 = queries[:, col + LANES : col + 2 * LANES]
            q2 = queries[:, col + 2 * LANES : col + 3 * LANES]
            even = slice(h * BLOCK, (h + 1) * BLOCK)
            odd = slice((h + 1) * BLOCK, (h + 2) * BLOCK)
            if g == 0:
                r1, r2 = rolled(q1), rolled(q2)
                near_queries[g, even, :LANES] = q0
                near_queries[g, even, LANES:] = jnp.where(low, q1, own_row)
                near_queries[g, odd, :LANES] = jnp.where(low, r1, r2)
                near_queries[g, odd, LANES:] = jnp.where(low, r2, own_row)
            else:
                r0, r1 = rolled(q0), rolled(q1)
                near_queries[g, even, :LANES] = jnp.where(low, own_row, r0)
                near_queries[g, even, LANES:] = jnp.where(low, r0, r1)
                near_queries[g, odd, :LANES] = jnp.where(low, own_row, q1)
                near_queries[g, odd, LANES:] = q2

    to_log2 = math.log2(math.e) / math.sqrt(D_HEAD)
    per_chunk = chunk // BLOCK

    def scores_of(g, i):
        return lax.dot_general(
            near_queries[g, i * chunk : (i + 1) * chunk, :],
            near_keys[g],
            (((1,), (1,)), ((), ())),
            preferred_element_type=jnp.float32,
        )

    todo = [(g, i) for g in range(groups) for i in range(heads_per // per_chunk)]
    ahead = scores_of(*todo[0])
    for n, (g, i) in enumerate(todo):
        scores = ahead
        if n + 1 < len(todo):
            ahead = scores_of(*todo[n + 1])
        row_max = jnp.max(scores, axis=1, keepdims=True)
        terms = jnp.exp2((scores - row_max) * to_log2).astype(jnp.bfloat16)
        summed = lax.dot_general(
            terms, near_values[g], (((1,), (0,)), ((), ())), preferred_element_type=jnp.float32
        )
        result = (summed[:, :D_VALUE] / summed[:, D_VALUE:]).astype(jnp.bfloat16)
        for k in range(per_chunk):
            col = (g * heads_per + i * per_chunk + k) * D_VALUE
            out[:, col : col + D_VALUE] = result[k * BLOCK : (k + 1) * BLOCK]


def attention(queries, key_pieces, value_pieces, picks, groups, slots):
    tok_rows, width = queries.shape
    heads_per = width // (groups * D_HEAD)
    pieces = len(key_pieces)
    steps = tok_rows // BLOCK
    out_width = groups * heads_per * D_VALUE
    body = functools.partial(
        attend_kernel, pieces=pieces, groups=groups, heads_per=heads_per, slots=slots, chunk=256
    )
    return pl.pallas_call(
        body,
        out_shape=jax.ShapeDtypeStruct((tok_rows, out_width), jnp.bfloat16),
        grid_spec=pltpu.PrefetchScalarGridSpec(
            num_scalar_prefetch=1,
            grid=(steps,),
            in_specs=[pl.BlockSpec((BLOCK, width), lambda b, _: (b, 0))]
            + [pl.BlockSpec(memory_space=pl.ANY)] * (2 * pieces),
            out_specs=pl.BlockSpec((BLOCK, out_width), lambda b, _: (b, 0)),
            scratch_shapes=[
                pltpu.VMEM((pieces, *key_pieces[0].shape), jnp.bfloat16),
                pltpu.VMEM((pieces, *value_pieces[0].shape), jnp.bfloat16),
                pltpu.VMEM((groups, slots * BLOCK, 2 * LANES), jnp.bfloat16),
                pltpu.VMEM((groups, slots * BLOCK, 2 * LANES), jnp.bfloat16),
                pltpu.VMEM((groups, heads_per * BLOCK, 2 * LANES), jnp.bfloat16),
                pltpu.SemaphoreType.DMA((2, pieces)),
            ],
        ),
        compiler_params=pltpu.CompilerParams(vmem_limit_bytes=60 * 1024 * 1024),
    )(picks, queries, *key_pieces, *value_pieces)


def per_device(queries, keys, values, selected, *, devices):
    groups = keys.shape[1] // D_HEAD
    slots = selected.shape[2]

    def swap(x, mask):
        return lax.ppermute(x, "ctx", [(i, i ^ mask) for i in range(devices)])

    key_pieces, value_pieces = {0: keys}, {0: values}
    for j in range(2, devices, 2):
        first, last = j & -j, 1 << (j.bit_length() - 1)
        key_pieces[j] = swap(key_pieces[j ^ last], last)
        value_pieces[j] = swap(value_pieces[j ^ first], first)
    for j in range(0, devices, 2):
        key_pieces[j + 1] = swap(key_pieces[j], 1)
        value_pieces[j + 1] = swap(value_pieces[j], 1)
    picks = jnp.concatenate([selected.reshape(-1), lax.axis_index("ctx").reshape(1).astype(jnp.int32)])
    order = range(devices)
    return attention(
        queries, [key_pieces[j] for j in order], [value_pieces[j] for j in order], picks, groups, slots
    )


def solution(mesh):
    return jax.shard_map(
        functools.partial(per_device, devices=mesh.shape["ctx"]),
        mesh=mesh,
        in_specs=(
            P(("batch", "ctx"), None),
            P(("batch", "ctx"), None),
            P(("batch", "ctx"), None),
            P(("batch", "ctx"), None, None),
        ),
        out_specs=P(("batch", "ctx"), None),
        check_vma=False,
    )
```

```python
import functools
import math

import jax
import jax.numpy as jnp
from jax import lax
from jax.experimental import pallas as pl
from jax.experimental.pallas import tpu as pltpu
from jax.sharding import PartitionSpec as P

D_HEAD = 192
D_VALUE = 128
BLOCK = 64
LANES = 128
HALF = 64
NEG = -1e30
TO_LOG2 = math.log2(math.e) / math.sqrt(D_HEAD)
VMEM_LIMIT = 60 * 1024 * 1024
VMEM_SPEC = pl.BlockSpec(memory_space=pltpu.VMEM)


def rolled(x):
    return pltpu.roll(x.astype(jnp.float32), HALF, 1).astype(jnp.bfloat16)


def low_lanes(rows):
    return lax.broadcasted_iota(jnp.int32, (rows, LANES), 1) < HALF


def pack_kernel(keys, values, first, second):
    rows = keys.shape[0]
    half = rows // 2
    low = low_lanes(half)
    top = keys[:half, LANES : 2 * LANES]
    bottom = keys[half:, LANES : 2 * LANES]
    first[:rows] = keys[:, :LANES]
    first[rows : rows + half] = jnp.where(low, top, rolled(bottom))
    first[rows + half :] = values[:, :D_VALUE]
    second[:rows] = keys[:, 2 * LANES :]
    second[rows : rows + half] = jnp.where(low, rolled(top), bottom)
    second[rows + half :] = values[:, D_VALUE:]


def pack(keys, values):
    rows = keys.shape[0]
    shape = jax.ShapeDtypeStruct((rows * 5 // 2, LANES), jnp.bfloat16)
    return pl.pallas_call(
        pack_kernel, out_shape=(shape, shape), in_specs=[VMEM_SPEC] * 2, out_specs=(VMEM_SPEC, VMEM_SPEC)
    )(keys, values)


def attend_kernel(picks, q_first, q_near, q_next, *refs, parts, group, first_block, heads_per, slots, chunk, aliased):
    count = sum(len(part) for part in parts)
    piece_refs = refs[:count]
    out, key_table, value_table, biases = refs[count + aliased : count + aliased + 4]
    near_keys, near_values, near_queries = (refs[count + aliased + 4 + 2 * n :][:2] for n in range(3))
    carried = refs[-1]
    step = pl.program_id(0)
    rows = value_table.shape[1]
    half = rows // 2
    blocks = rows // BLOCK
    low = low_lanes(BLOCK)
    lane = lax.broadcasted_iota(jnp.int32, (BLOCK, LANES), 1) % HALF
    row = lax.broadcasted_iota(jnp.int32, (BLOCK, LANES), 0)
    own_row = (lane == row).astype(jnp.bfloat16)
    my_index = picks[picks.shape[0] - 1]
    groups = (picks.shape[0] - 1) // (blocks * slots)
    flipped = group % 2 == 1

    def fill_tables():
        n = 0
        for j, part in enumerate(parts):
            at = 0
            for size in part:
                piece, end = piece_refs[n], at + size
                n += 1
                a, b = at, min(end, rows)
                if a < b:
                    key_table[j, a:b, (LANES if flipped else 0) : (2 * LANES if flipped else LANES)] = piece[a - at : b - at]
                a, b = max(at, rows), min(end, rows + half)
                if a < b:
                    pair = piece[a - at : b - at]
                    other = rolled(pair)
                    low_pair = low_lanes(b - a)
                    zero = jnp.zeros_like(pair)
                    side = slice(0, LANES) if flipped else slice(LANES, 2 * LANES)
                    upper, lower = (pair, other) if flipped else (other, pair)
                    keep = jnp.logical_not(low_pair) if flipped else low_pair
                    key_table[j, a - rows : b - rows, side] = jnp.where(keep, lower, zero)
                    key_table[j, a - half : b - half, side] = jnp.where(keep, upper, zero)
                a, b = max(at, rows + half), end
                if a < b:
                    value_table[j, a - rows - half : b - rows - half] = piece[a - at : b - at]
                at = end
        biases[0] = jnp.zeros((BLOCK, LANES), jnp.bfloat16)
        biases[1] = jnp.where(row > lane, NEG, 0.0).astype(jnp.bfloat16)
        biases[2] = jnp.full((BLOCK, LANES), NEG, jnp.bfloat16)
        for values in near_values:
            values[:, D_VALUE:] = jnp.ones((slots * BLOCK, LANES), jnp.bfloat16)

    def gather(b, buf):
        keys, values = near_keys[buf], near_values[buf]
        for s in range(slots):
            pick = picks[(b * groups + group) * slots + s]
            listed = jnp.maximum(pick, 0)
            piece = (listed // blocks) ^ my_index
            at = pl.ds(pl.multiple_of((listed % blocks) * BLOCK, BLOCK), BLOCK)
            kind = jnp.where(pick == my_index * blocks + b, 1, jnp.where(pick < 0, 2, 0))
            to = slice(s * BLOCK, (s + 1) * BLOCK)
            if flipped:
                keys[to, :LANES] = jnp.where(low, biases[kind], key_table[piece, at, :LANES])
                keys[to, LANES:] = key_table[piece, at, LANES:]
            else:
                keys[to, :LANES] = key_table[piece, at, :LANES]
                keys[to, LANES:] = jnp.where(low, key_table[piece, at, LANES:], biases[kind])
            values[to, :D_VALUE] = value_table[piece, at, :]

    def place(q_ref, buf):
        to = near_queries[buf]
        for h in range(0, heads_per, 2):
            col = h * D_HEAD
            q0 = q_ref[:, col : col + LANES]
            q1 = q_ref[:, col + LANES : col + 2 * LANES]
            q2 = q_ref[:, col + 2 * LANES : col + 3 * LANES]
            even = slice(h * BLOCK, (h + 1) * BLOCK)
            odd = slice((h + 1) * BLOCK, (h + 2) * BLOCK)
            if flipped:
                r0, r1 = rolled(q0), rolled(q1)
                to[even, :LANES] = jnp.where(low, own_row, r0)
                to[even, LANES:] = jnp.where(low, r0, r1)
                to[odd, :LANES] = jnp.where(low, own_row, q1)
                to[odd, LANES:] = q2
            else:
                r1, r2 = rolled(q1), rolled(q2)
                to[even, :LANES] = q0
                to[even, LANES:] = jnp.where(low, q1, own_row)
                to[odd, :LANES] = jnp.where(low, r1, r2)
                to[odd, LANES:] = jnp.where(low, r2, own_row)

    def scores_of(buf, i):
        return lax.dot_general(
            near_queries[buf][i * chunk : (i + 1) * chunk, :],
            near_keys[buf][...],
            (((1,), (1,)), ((), ())),
            preferred_element_type=jnp.float32,
        )

    @pl.when(step == 0)
    def _():
        fill_tables()
        gather(first_block, 0)
        place(q_first, 0)
        carried[...] = scores_of(0, 0)

    last = first_block + 2 * pl.num_programs(0) - 1
    per_chunk = chunk // BLOCK
    chunks = heads_per // per_chunk
    scores = carried[...]
    for buf in range(2):
        after = jnp.minimum(first_block + 2 * step + buf + 1, last)
        for i in range(chunks):
            if i == 0:
                gather(after, 1 - buf)
                place((q_near, q_next)[buf], 1 - buf)
            ahead = scores_of(buf, i + 1) if i + 1 < chunks else scores_of(1 - buf, 0)
            if buf == 1 and i + 1 == chunks:
                carried[...] = ahead
            row_max = jnp.max(scores, axis=1, keepdims=True)
            terms = jnp.exp2((scores - row_max) * TO_LOG2).astype(jnp.bfloat16)
            summed = lax.dot_general(
                terms, near_values[buf][...], (((1,), (0,)), ((), ())), preferred_element_type=jnp.float32
            )
            result = (summed[:, :D_VALUE] / summed[:, D_VALUE:]).astype(jnp.bfloat16)
            for k in range(per_chunk):
                col = (i * per_chunk + k) * D_VALUE
                out[buf * BLOCK : (buf + 1) * BLOCK, col : col + D_VALUE] = result[k * BLOCK : (k + 1) * BLOCK]
            scores = ahead


def attend(queries, pieces, picks, so_far, *, group, groups, slots, first_block, blocks, chunk=256):
    tok_rows, width = queries.shape
    heads_per = width // (groups * D_HEAD)
    group_width = heads_per * D_HEAD
    group_out = heads_per * D_VALUE
    parts = tuple(tuple(a.shape[0] for a in p) for p in pieces)
    flat = [a for p in pieces for a in p]
    aliased = 0 if so_far is None else 1
    last = first_block + blocks - 1
    body = functools.partial(
        attend_kernel, parts=parts, group=group, first_block=first_block, heads_per=heads_per, slots=slots,
        chunk=chunk, aliased=aliased,
    )
    return pl.pallas_call(
        body,
        out_shape=jax.ShapeDtypeStruct((tok_rows, groups * group_out), jnp.bfloat16),
        grid_spec=pltpu.PrefetchScalarGridSpec(
            num_scalar_prefetch=1,
            grid=(blocks // 2,),
            in_specs=[
                pl.BlockSpec((BLOCK, group_width), lambda b, _: (first_block, group), pipeline_mode=pl.Buffered(1)),
                pl.BlockSpec((BLOCK, group_width), lambda b, _: (first_block + 2 * b + 1, group)),
                pl.BlockSpec((BLOCK, group_width), lambda b, _: (jnp.minimum(first_block + 2 * b + 2, last), group)),
            ]
            + [VMEM_SPEC] * len(flat)
            + [pl.BlockSpec(memory_space=pl.ANY)] * aliased,
            out_specs=pl.BlockSpec((2 * BLOCK, group_out), lambda b, _: (b + first_block // 2, group)),
            scratch_shapes=[
                pltpu.VMEM((len(pieces), tok_rows, 2 * LANES), jnp.bfloat16),
                pltpu.VMEM((len(pieces), tok_rows, D_VALUE), jnp.bfloat16),
                pltpu.VMEM((3, BLOCK, LANES), jnp.bfloat16),
            ]
            + [pltpu.VMEM((slots * BLOCK, 2 * LANES), jnp.bfloat16)] * 4
            + [pltpu.VMEM((heads_per * BLOCK, 2 * LANES), jnp.bfloat16)] * 2
            + [pltpu.VMEM((chunk, slots * BLOCK), jnp.float32)],
        ),
        input_output_aliases={4 + len(flat): 0} if aliased else {},
        compiler_params=pltpu.CompilerParams(vmem_limit_bytes=VMEM_LIMIT),
    )(picks, queries, queries, queries, *flat, *([so_far] if aliased else []))


def per_device(queries, keys, values, selected, *, devices):
    groups = keys.shape[1] // D_HEAD
    slots = selected.shape[2]
    blocks = selected.shape[0]
    picks = jnp.concatenate([selected.reshape(-1), lax.axis_index("ctx").reshape(1).astype(jnp.int32)])

    def swap(x, mask):
        return lax.ppermute(x, "ctx", [(i, i ^ mask) for i in range(devices)])

    chunks = pack(keys, values)
    result = None
    for g in range(groups):
        pieces = {0: (chunks[g],)}
        split = chunks[g].shape[0] // 2
        for j in range(2, devices, 2):
            low, high = j & -j, 1 << (j.bit_length() - 1)
            if low == high:
                pieces[j] = (swap(chunks[g], j),)
            else:
                a = jnp.concatenate(pieces[j ^ high])[:split]
                b = jnp.concatenate(pieces[j ^ low])[split:]
                pieces[j] = (swap(a, high), swap(b, low))
        for j in range(0, devices, 2):
            pieces[j + 1] = tuple(swap(a, 1) for a in pieces[j])
        result = attend(
            queries, [pieces[j] for j in range(devices)], picks, result,
            group=g, groups=groups, slots=slots, first_block=0, blocks=blocks,
        )
    return result


def solution(mesh):
    return jax.shard_map(
        functools.partial(per_device, devices=mesh.shape["ctx"]),
        mesh=mesh,
        in_specs=(
            P(("batch", "ctx"), None),
            P(("batch", "ctx"), None),
            P(("batch", "ctx"), None),
            P(("batch", "ctx"), None, None),
        ),
        out_specs=P(("batch", "ctx"), None),
        check_vma=False,
    )
```

```python
import functools
import math

import jax
import jax.numpy as jnp
from jax import lax
from jax.experimental import pallas as pl
from jax.experimental.pallas import tpu as pltpu
from jax.sharding import PartitionSpec as P


D_HEAD = 192
D_VALUE = 128
BLOCK = 64
LANES = 128
HALF = 64
NEG = -1e30
TO_LOG2 = math.log2(math.e) / math.sqrt(D_HEAD)
MIB = 1024 * 1024
VMEM_SPEC = pl.BlockSpec(memory_space=pltpu.VMEM)


def rolled(x):
    return pltpu.roll(x.astype(jnp.float32), HALF, 1).astype(jnp.bfloat16)


def low_lanes(rows):
    return lax.broadcasted_iota(jnp.int32, (rows, LANES), 1) < HALF


def pack_kernel(keys, values, first, second):
    rows = keys.shape[0]
    half = rows // 2
    low = low_lanes(half)
    top = keys[:half, LANES : 2 * LANES]
    bottom = keys[half:, LANES : 2 * LANES]
    first[:rows] = keys[:, :LANES]
    first[rows : rows + half] = jnp.where(low, top, rolled(bottom))
    first[rows + half :] = values[:, :D_VALUE]
    second[:rows] = keys[:, 2 * LANES :]
    second[rows : rows + half] = jnp.where(low, rolled(top), bottom)
    second[rows + half :] = values[:, D_VALUE:]


def pack(keys, values):
    rows = keys.shape[0]
    shape = pltpu.VMEM((rows * 5 // 2, LANES), jnp.bfloat16)
    return pl.pallas_call(
        pack_kernel,
        out_shape=(shape, shape),
        in_specs=[VMEM_SPEC] * 2,
        out_specs=(VMEM_SPEC, VMEM_SPEC),
        compiler_params=pltpu.CompilerParams(vmem_limit_bytes=4 * MIB),
    )(keys, values)


def place_kernel(queries, *placed, heads_per):
    step = pl.program_id(0)
    low = low_lanes(BLOCK)
    lane = lax.broadcasted_iota(jnp.int32, (BLOCK, LANES), 1) % HALF
    own_row = (lane == lax.broadcasted_iota(jnp.int32, (BLOCK, LANES), 0)).astype(jnp.bfloat16)
    for g, to in enumerate(placed):
        for h in range(0, heads_per, 2):
            col = (g * heads_per + h) * D_HEAD
            q0 = queries[:, col : col + LANES]
            q1 = queries[:, col + LANES : col + 2 * LANES]
            q2 = queries[:, col + 2 * LANES : col + 3 * LANES]
            even = pl.ds(pl.multiple_of((step * heads_per + h) * BLOCK, BLOCK), BLOCK)
            odd = pl.ds(pl.multiple_of((step * heads_per + h + 1) * BLOCK, BLOCK), BLOCK)
            if g % 2:
                r0, r1 = rolled(q0), rolled(q1)
                to[even, :LANES] = jnp.where(low, own_row, r0)
                to[even, LANES:] = jnp.where(low, r0, r1)
                to[odd, :LANES] = jnp.where(low, own_row, q1)
                to[odd, LANES:] = q2
            else:
                r1, r2 = rolled(q1), rolled(q2)
                to[even, :LANES] = q0
                to[even, LANES:] = jnp.where(low, q1, own_row)
                to[odd, :LANES] = jnp.where(low, r1, r2)
                to[odd, LANES:] = jnp.where(low, r2, own_row)


def place(queries, groups):
    tok_rows, width = queries.shape
    heads_per = width // (groups * D_HEAD)
    shape = pltpu.VMEM((tok_rows * heads_per, 2 * LANES), jnp.bfloat16)
    return pl.pallas_call(
        functools.partial(place_kernel, heads_per=heads_per),
        out_shape=(shape,) * groups,
        grid=(tok_rows // BLOCK,),
        in_specs=[pl.BlockSpec((BLOCK, width), lambda b: (b, 0))],
        out_specs=(VMEM_SPEC,) * groups,
        compiler_params=pltpu.CompilerParams(vmem_limit_bytes=8 * MIB),
    )(queries)


def attend_kernel(picks, queries, *refs, parts, group, heads_per, chunk, aliased):
    count = sum(len(part) for part in parts)
    piece_refs = refs[:count]
    out, key_table, value_table, biases = refs[count + aliased : count + aliased + 4]
    near_keys, near_values = (refs[count + aliased + 4 + 2 * n :][:2] for n in range(2))
    carried = refs[-1]
    step = pl.program_id(0)
    blocks, _, slots = picks.shape
    rows = value_table.shape[1]
    half = rows // 2
    low = low_lanes(BLOCK)
    lane = lax.broadcasted_iota(jnp.int32, (BLOCK, LANES), 1) % HALF
    row = lax.broadcasted_iota(jnp.int32, (BLOCK, LANES), 0)
    my_index = lax.axis_index("ctx")
    flipped = group % 2 == 1

    def fill_tables():
        n = 0
        for j, part in enumerate(parts):
            at = 0
            for size in part:
                piece, end = piece_refs[n], at + size
                n += 1
                a, b = at, min(end, rows)
                if a < b:
                    key_table[j, a:b, (LANES if flipped else 0) : (2 * LANES if flipped else LANES)] = piece[a - at : b - at]
                a, b = max(at, rows), min(end, rows + half)
                if a < b:
                    pair = piece[a - at : b - at]
                    other = rolled(pair)
                    low_pair = low_lanes(b - a)
                    zero = jnp.zeros_like(pair)
                    side = slice(0, LANES) if flipped else slice(LANES, 2 * LANES)
                    upper, lower = (pair, other) if flipped else (other, pair)
                    keep = jnp.logical_not(low_pair) if flipped else low_pair
                    key_table[j, a - rows : b - rows, side] = jnp.where(keep, lower, zero)
                    key_table[j, a - half : b - half, side] = jnp.where(keep, upper, zero)
                a, b = max(at, rows + half), end
                if a < b:
                    value_table[j, a - rows - half : b - rows - half] = piece[a - at : b - at]
                at = end
        biases[0] = jnp.zeros((BLOCK, LANES), jnp.bfloat16)
        biases[1] = jnp.where(row > lane, NEG, 0.0).astype(jnp.bfloat16)
        biases[2] = jnp.full((BLOCK, LANES), NEG, jnp.bfloat16)
        for values in near_values:
            values[:, D_VALUE:] = jnp.ones((slots * BLOCK, LANES), jnp.bfloat16)

    def gather(b, buf):
        keys, values = near_keys[buf], near_values[buf]
        for s in range(slots):
            pick = picks[b, group, s]
            listed = jnp.maximum(pick, 0)
            piece = (listed // blocks) ^ my_index
            at = pl.ds(pl.multiple_of((listed % blocks) * BLOCK, BLOCK), BLOCK)
            kind = jnp.where(pick == my_index * blocks + b, 1, jnp.where(pick < 0, 2, 0))
            to = slice(s * BLOCK, (s + 1) * BLOCK)
            if flipped:
                keys[to, :LANES] = jnp.where(low, biases[kind], key_table[piece, at, :LANES])
                keys[to, LANES:] = key_table[piece, at, LANES:]
            else:
                keys[to, :LANES] = key_table[piece, at, :LANES]
                keys[to, LANES:] = jnp.where(low, key_table[piece, at, LANES:], biases[kind])
            values[to, :D_VALUE] = value_table[piece, at, :]

    def scores_of(b, buf, i):
        at = pl.multiple_of((b * heads_per) * BLOCK + i * chunk, chunk)
        return lax.dot_general(
            queries[pl.ds(at, chunk), :],
            near_keys[buf][...],
            (((1,), (1,)), ((), ())),
            preferred_element_type=jnp.float32,
        )

    @pl.when(step == 0)
    def _():
        fill_tables()
        gather(0, 0)
        carried[...] = scores_of(0, 0, 0)

    per_chunk = chunk // BLOCK
    chunks = heads_per // per_chunk
    scores = carried[...]
    for buf in range(2):
        now = 2 * step + buf
        after = jnp.minimum(now + 1, blocks - 1)
        for i in range(chunks):
            if i == 0:
                gather(after, 1 - buf)
            ahead = scores_of(now, buf, i + 1) if i + 1 < chunks else scores_of(after, 1 - buf, 0)
            if buf == 1 and i + 1 == chunks:
                carried[...] = ahead
            row_max = jnp.max(scores, axis=1, keepdims=True)
            terms = jnp.exp2((scores - row_max) * TO_LOG2).astype(jnp.bfloat16)
            summed = lax.dot_general(
                terms, near_values[buf][...], (((1,), (0,)), ((), ())), preferred_element_type=jnp.float32
            )
            result = (summed[:, :D_VALUE] / summed[:, D_VALUE:]).astype(jnp.bfloat16)
            for k in range(per_chunk):
                col = (i * per_chunk + k) * D_VALUE
                out[buf * BLOCK : (buf + 1) * BLOCK, col : col + D_VALUE] = result[k * BLOCK : (k + 1) * BLOCK]
            scores = ahead


def attend(queries, pieces, picks, so_far, *, group, chunk=256):
    blocks, groups, slots = picks.shape
    tok_rows = blocks * BLOCK
    heads_per = queries.shape[0] // tok_rows
    group_out = heads_per * D_VALUE
    parts = tuple(tuple(a.shape[0] for a in p) for p in pieces)
    flat = [pltpu.with_memory_space_constraint(a, pltpu.VMEM) for p in pieces for a in p]
    queries = pltpu.with_memory_space_constraint(queries, pltpu.VMEM)
    aliased = 0 if so_far is None else 1
    table_bytes = len(pieces) * tok_rows * (2 * LANES + D_VALUE) * 2
    return pl.pallas_call(
        functools.partial(
            attend_kernel, parts=parts, group=group, heads_per=heads_per, chunk=chunk, aliased=aliased
        ),
        out_shape=jax.ShapeDtypeStruct((tok_rows, groups * group_out), jnp.bfloat16),
        grid_spec=pltpu.PrefetchScalarGridSpec(
            num_scalar_prefetch=1,
            grid=(blocks // 2,),
            in_specs=[VMEM_SPEC] * (1 + len(flat)) + [pl.BlockSpec(memory_space=pl.ANY)] * aliased,
            out_specs=pl.BlockSpec((2 * BLOCK, group_out), lambda b, _: (b, group)),
            scratch_shapes=[
                pltpu.VMEM((len(pieces), tok_rows, 2 * LANES), jnp.bfloat16),
                pltpu.VMEM((len(pieces), tok_rows, D_VALUE), jnp.bfloat16),
                pltpu.VMEM((3, BLOCK, LANES), jnp.bfloat16),
            ]
            + [pltpu.VMEM((slots * BLOCK, 2 * LANES), jnp.bfloat16)] * 4
            + [pltpu.VMEM((chunk, slots * BLOCK), jnp.float32)],
        ),
        input_output_aliases={2 + len(flat): 0} if aliased else {},
        compiler_params=pltpu.CompilerParams(vmem_limit_bytes=16 * MIB + 2 * table_bytes),
    )(picks, queries, *flat, *([so_far] if aliased else []))


def per_device(queries, keys, values, selected, *, devices):
    groups = keys.shape[1] // D_HEAD

    def swap(x, mask):
        return lax.ppermute(x, "ctx", [(i, i ^ mask) for i in range(devices)])

    chunks = pack(keys, values)
    placed = place(queries, groups)
    result = None
    for g in range(groups):
        chunk = chunks[g]
        split = chunk.shape[0] // 2
        pieces = {0: (chunk,)}
        for j in range(2, devices, 2):
            low, high = j & -j, 1 << (j.bit_length() - 1)
            if g > 0 or low == high:
                pieces[j] = (swap(chunk, j),)
            else:
                a = jnp.concatenate(pieces[j ^ high])[:split]
                b = jnp.concatenate(pieces[j ^ low])[split:]
                pieces[j] = (swap(a, high), swap(b, low))
        for j in range(0, devices, 2):
            pieces[j + 1] = tuple(swap(a, 1) for a in pieces[j])
        result = attend(placed[g], [pieces[j] for j in range(devices)], selected, result, group=g)
    return result


def solution(mesh):
    devices = mesh.shape["ctx"]
    return jax.shard_map(
        functools.partial(per_device, devices=devices),
        mesh=mesh,
        in_specs=(
            P(("batch", "ctx"), None),
            P(("batch", "ctx"), None),
            P(("batch", "ctx"), None),
            P(("batch", "ctx"), None, None),
        ),
        out_specs=P(("batch", "ctx"), None),
        check_vma=False,
    )
```
